32 devices in a mesh: lat: 4 (over y, x), lon: 8 (over z, core).
Axes of the slice: x: 2, y: 2, z: 4, core: 2. Of those that a mesh axis runs over, the one named last changes fastest.
Arguments:
- departures: bfloat16 [65536, 256], P(('lat', 'lon')), may hold values from -6 to 6
- footprint: int32 [65536, 4], P(('lat', 'lon')), may hold values from 0 to 131071, as said below
- channel_map: bfloat16 [256, 128], replicated, may hold values from -0.375 to 0.375
- adjoint_in: float32 [128, 128, 1024], P(None, 'lat', 'lon'), may hold values from -6 to 6
- wind_lon: float32 [128, 128, 1024], P(None, 'lat', 'lon'), may hold values from -0.4 to 0.4
- wind_lat: float32 [128, 128, 1024], P(None, 'lat', 'lon'), may hold values from -0.4 to 0.4
Outputs:
- adjoint_out: float32 [128, 128, 1024], P(None, 'lat', 'lon')
The draws below stay inside these ranges and needn't reach their ends.
Inputs may be any that keep to these rules, and one draw needn't show every extreme that they name: `footprint`: the 4 columns of an observation form a 2 by 2 block of neighbouring columns that lie in one device's block of 32 x 128 columns (wrapping inside that block). The observations of one holder device fall into at most 128 per owner device, and in every holder's rows some owner device receives exactly 128.
All inputs are finite; a program needn't handle non-finite values.
Results may differ from the reference program's by a relative error of at most 0.0015.
Values may be sent and summed in bfloat16 or wider, within the bound.
A program may use at most 64 MiB of HBM per device.

```python
import jax
import jax.numpy as jnp
from jax import lax

CH = 256
LEV = 128
FOOT = 4
STEPS = 2
CLAT = 32
CLON = 128
OBS_DEV = 2048
CAP = 128
NLAT = 128
NLON = 1024
OBS = 65536
N_LON = 8
DEVICES = 32


def draw_footprint(key, part):
    slot_count = DEVICES * CAP
    key_noise = jax.random.fold_in(key, 11)
    key_weight = jax.random.fold_in(key, 12)
    key_hot = jax.random.fold_in(key, 13)
    key_shuffle = jax.random.fold_in(key, 14)
    key_row = jax.random.fold_in(key, 15)
    key_col = jax.random.fold_in(key, 16)
    slot_noise = jax.random.randint(key_noise, (DEVICES, slot_count), 0, 2 ** 15)
    owner_weight = jax.random.randint(key_weight, (DEVICES,), 0, 4)
    hot_owner = jax.random.randint(key_hot, (DEVICES, 1), 0, DEVICES)
    slot_owner = jnp.arange(slot_count, dtype=jnp.int32) // CAP
    slot_score = slot_noise + owner_weight[slot_owner][None, :] * 2 ** 13
    slot_score = slot_score + jnp.where(slot_owner[None, :] == hot_owner, 2 ** 17, 0)
    slot_score = slot_score * 4096 + jnp.arange(slot_count, dtype=jnp.int32)[None, :]
    chosen = lax.top_k(slot_score, OBS_DEV)[1]
    shuffle_score = jax.random.randint(key_shuffle, (DEVICES, OBS_DEV), 0, 2 ** 18) * 4096
    shuffle_score = shuffle_score + jnp.arange(OBS_DEV, dtype=jnp.int32)[None, :]
    order = jnp.argsort(shuffle_score, axis=1, stable=True)
    chosen = jnp.take_along_axis(chosen, order, axis=1)
    owner_index = chosen // CAP
    owner_lat = owner_index // N_LON
    owner_lon = owner_index % N_LON
    row_base = jax.random.randint(key_row, (DEVICES, OBS_DEV), 0, CLAT)
    col_base = jax.random.randint(key_col, (DEVICES, OBS_DEV), 0, CLON)
    pieces = []
    for row_step, col_step in ((0, 0), (0, 1), (1, 0), (1, 1)):
        grid_lat = owner_lat * CLAT + (row_base + row_step) % CLAT
        grid_lon = owner_lon * CLON + (col_base + col_step) % CLON
        pieces.append(grid_lat * NLON + grid_lon)
    return jnp.stack(pieces, -1).reshape(OBS, FOOT).astype(jnp.int32)


def block_levels(stream_key, extent, cuts, least, high):
    loudness, own = 1.0, jax.random.fold_in(stream_key, 6)
    for dim, shards_of in cuts:
        heights = jnp.exp(jax.random.uniform(jax.random.fold_in(own, dim), (shards_of,), jnp.float32, least / len(cuts), high / len(cuts)))
        loudness = loudness * jnp.repeat(heights, extent[dim] // shards_of).reshape([-1 if axis == dim else 1 for axis in range(len(extent))])
    return loudness


def noise(stream_key, extent, width, limit, cuts=(), held_as=jnp.bfloat16):
    drawn = jax.random.normal(stream_key, extent, jnp.float32) * width
    if len(cuts) > 0:
        drawn = block_levels(stream_key, extent, cuts, -0.22, 0.18) * drawn
    return jnp.clip(drawn, min=-limit, max=limit).astype(held_as)


def setup_inputs(seed: int = 0) -> dict:
    streams_of = jax.random.split(jax.random.key(seed), 7)
    departures = noise(streams_of[0], (OBS, CH), 1.0, 6.0, ((0, 32),))
    footprint = draw_footprint(jax.random.fold_in(streams_of[6], 71), 0)
    channel_map = noise(streams_of[2], (CH, LEV), CH ** -0.5, 0.375)
    adjoint_in = noise(streams_of[3], (LEV, NLAT, NLON), 1.0, 6.0, ((1, 4), (2, 8)), jnp.float32)
    wind_lon = jnp.clip(jax.random.uniform(streams_of[4], (LEV, NLAT, NLON), jnp.float32, -0.4, 0.4) * block_levels(streams_of[4], (LEV, NLAT, NLON), ((1, 4), (2, 8)), -0.4, 0.0), -0.4, 0.4)
    wind_lat = jnp.clip(jax.random.uniform(streams_of[5], (LEV, NLAT, NLON), jnp.float32, -0.4, 0.4) * block_levels(streams_of[5], (LEV, NLAT, NLON), ((1, 4), (2, 8)), -0.4, 0.0), -0.4, 0.4)
    return dict(departures=departures, footprint=footprint, channel_map=channel_map, adjoint_in=adjoint_in, wind_lon=wind_lon, wind_lat=wind_lat)


diffusion_rate = 0.2


def deposit_profiles(profiles, columns, column_count):
    values = profiles.astype(jnp.float32)
    deposit = jnp.zeros((column_count, values.shape[1]), jnp.float32)
    for corner in range(FOOT):
        deposit = deposit + jax.ops.segment_sum(values, columns[:, corner], num_segments=column_count)
    return deposit * 0.25


def lon_sides(field):
    return jnp.roll(field, -1, 2), jnp.roll(field, 1, 2)


def lat_sides(field):
    padded = jnp.pad(field, ((0, 0), (1, 1), (0, 0)))
    return padded[:, 2:, :], padded[:, :-2, :]


def adjoint_step(adjoint_state, wind_lon, wind_lat):
    east_side, west_side = lon_sides(adjoint_state)
    north_side, south_side = lat_sides(adjoint_state)
    east_flux, west_flux = lon_sides(wind_lon * adjoint_state)
    north_flux, south_flux = lat_sides(wind_lat * adjoint_state)
    laplace = east_side + west_side + north_side + south_side - 4.0 * adjoint_state
    return adjoint_state + diffusion_rate * laplace + 0.5 * (east_flux - west_flux) + 0.5 * (north_flux - south_flux)


def reference(departures, footprint, channel_map, adjoint_in, wind_lon, wind_lat):
    profiles = jnp.dot(departures, channel_map, preferred_element_type=jnp.float32).astype(jnp.bfloat16)
    deposit = deposit_profiles(profiles, footprint, NLAT * NLON)
    adjoint_state = adjoint_in + deposit.T.reshape(LEV, NLAT, NLON)
    for advect_step in range(STEPS):
        adjoint_state = adjoint_step(adjoint_state, wind_lon, wind_lat)
    return adjoint_state
```

```python
import functools

import jax
import jax.numpy as jnp
from jax import lax
from jax.experimental import pallas as pl
from jax.experimental.pallas import tpu as pltpu
from jax.sharding import PartitionSpec as P

STEPS = 2
RATE = 0.2
LANES = 128
META = 16
MESH = pl.DeviceIdType.MESH


def log2(size):
    assert size & (size - 1) == 0
    return size.bit_length() - 1


def nt_dot(a, b):
    return lax.dot_general(a, b, (((1,), (1,)), ((), ())), preferred_element_type=jnp.float32)


def kernel(
    n_lat, n_lon, foot, dep, cmap, adj_hbm, wlon_hbm, wlat_hbm, out_hbm,
    prof, tag, send, recv, state, later, wlon, wlat, edge_out, edge_in,
    load_sem, out_sem, send_sem, recv_sem, edge_send_sem, edge_recv_sem,
):
    lat, lon = lax.axis_index("lat"), lax.axis_index("lon")
    n_dev = n_lat * n_lon
    rows, levels, cols = state.shape
    obs = dep.shape[0]
    slots = recv.shape[2]

    barrier = pltpu.get_barrier_semaphore()

    def greet(i, carry):
        pl.semaphore_signal(
            barrier, inc=1,
            device_id=((lat + i // n_lon) % n_lat, (lon + i % n_lon) % n_lon),
            device_id_type=MESH,
        )
        return carry

    lax.fori_loop(1, n_dev, greet, 0)

    def load(r, carry):
        pltpu.make_async_copy(adj_hbm.at[:, r, :], state.at[r], load_sem.at[0]).start()
        pltpu.make_async_copy(wlon_hbm.at[:, r, :], wlon.at[r], load_sem.at[1]).start()
        pltpu.make_async_copy(wlat_hbm.at[:, r, :], wlat.at[r], load_sem.at[2]).start()
        return carry

    lax.fori_loop(0, rows, load, 0)

    shift_grid, shift_row, shift_col = log2(n_lon * cols), log2(rows), log2(cols)
    cells = foot[...]
    grid_row = lax.shift_right_logical(cells, shift_grid)
    grid_col = cells & (n_lon * cols - 1)
    owner = (
        lax.shift_right_logical(grid_row[0:1], shift_row) * n_lon
        + lax.shift_right_logical(grid_col[0:1], shift_col)
    )
    in_row = grid_row & (rows - 1)
    in_col = grid_col & (cols - 1)

    def base(cell):
        low = jnp.minimum(jnp.minimum(cell[0:1], cell[1:2]), jnp.minimum(cell[2:3], cell[3:4]))
        high = jnp.maximum(jnp.maximum(cell[0:1], cell[1:2]), jnp.maximum(cell[2:3], cell[3:4]))
        return jnp.where(high - low == 1, low, high)

    base_row, base_col = base(in_row), base(in_col)
    chunk = 256
    upper = jnp.where(
        lax.broadcasted_iota(jnp.int32, (chunk, chunk), 0)
        <= lax.broadcasted_iota(jnp.int32, (chunk, chunk), 1),
        1.0, 0.0,
    ).astype(jnp.bfloat16)
    owners = lax.broadcasted_iota(jnp.int32, (n_dev, chunk), 0)
    seen = jnp.zeros((n_dev, 1), jnp.float32)
    for start in range(0, obs, chunk):
        hot = jnp.where(owners == owner[:, start:start + chunk], 1.0, 0.0)
        count = jnp.dot(hot.astype(jnp.bfloat16), upper, preferred_element_type=jnp.float32) + seen
        place = jnp.sum(hot * count, axis=0, keepdims=True) - 1.0
        seen = count[:, chunk - 1:chunk]
        tag[0:1, start:start + chunk] = place.astype(jnp.int32)
    tag[1:2, :] = owner

    prof[0:levels, :] = nt_dot(cmap[...], dep[...]).astype(jnp.bfloat16)
    which = lax.broadcasted_iota(jnp.int32, (META, obs), 0)
    prof[levels:levels + META, :] = jnp.where(
        which == 0, base_row, jnp.where(which == 1, base_col, 0)
    ).astype(jnp.float32).astype(jnp.bfloat16)

    pl.semaphore_wait(barrier, n_dev - 1)

    def away(k):
        step = (k + 1) // 2
        return (n_lon // 2 + n_lon + step * (1 - 2 * (k % 2))) % n_lon

    def transfer(i, a, k):
        return pltpu.make_async_remote_copy(
            src_ref=send.at[i], dst_ref=recv.at[i],
            send_sem=send_sem.at[i], recv_sem=recv_sem.at[i],
            device_id=((lat + a) % n_lat, (lon + away(k)) % n_lon),
            device_id_type=MESH,
        )

    def route(k, carry):
        place, owner = tag[0:1, :], tag[1:2, :]
        slot = lax.broadcasted_iota(jnp.int32, (slots, obs), 0)
        hots = []
        for a in range(n_lat):
            target = (lat + a) % n_lat * n_lon + (lon + away(k)) % n_lon
            wanted = jnp.where(owner == target, place, -1)
            hots.append(jnp.where(slot == wanted, 1.0, 0.0).astype(jnp.bfloat16))
        blocks = nt_dot(prof[...], jnp.concatenate(hots, axis=0)).astype(jnp.bfloat16)
        for a in range(n_lat):
            i = k * n_lat + a
            block = blocks[:, a * slots:(a + 1) * slots]
            if a == 0:
                @pl.when(k == n_lon - 1)
                def _():
                    recv[i] = block

                @pl.when(k < n_lon - 1)
                def _():
                    send[i] = block
                    transfer(i, a, k).start()
            else:
                send[i] = block
                transfer(i, a, k).start()
        return carry

    lax.fori_loop(0, n_lon, route, 0)

    for which, buf in enumerate((state, wlon, wlat)):
        pltpu.make_async_copy(buf, buf, load_sem.at[which]).wait()

    tile = 8
    depth = n_lat * slots

    def deposit(k, carry):
        for a in range(n_lat):
            if a == 0:
                @pl.when(k < n_lon - 1)
                def _():
                    transfer(k * n_lat, 0, k).wait_recv()
            else:
                transfer(k * n_lat + a, a, k).wait_recv()
        parts = [recv[k * n_lat + a] for a in range(n_lat)]
        got = jnp.concatenate([p[0:levels] for p in parts], axis=1)
        meta = jnp.concatenate([p[levels:levels + META] for p in parts], axis=1)
        meta = meta.astype(jnp.float32).astype(jnp.int32)
        at_row, at_col = meta[0:1], meta[1:2]
        col = lax.broadcasted_iota(jnp.int32, (cols, depth), 0)
        col_hot = jnp.where(
            (col == at_col) | (col == ((at_col + 1) & (cols - 1))), 0.25, 0.0
        ).astype(jnp.bfloat16)
        next_row = (at_row + 1) & (rows - 1)
        stacked = got.reshape(levels // 16, 16, depth)

        def rows_of(t, carry):
            lhs = []
            for j in range(tile):
                r = t * tile + j
                hot = jnp.where((at_row == r) | (next_row == r), 1.0, 0.0)
                hot = jnp.broadcast_to(hot, (16, depth)).astype(jnp.bfloat16)
                lhs.append((stacked * hot[None]).reshape(levels, depth))
            out = nt_dot(jnp.concatenate(lhs, axis=0), col_hot)
            at = pl.ds(t * tile, tile)
            state[at] = state[at] + out.reshape(tile, levels, cols)
            return carry

        lax.fori_loop(0, rows // tile, rows_of, 0)
        return carry

    lax.fori_loop(0, n_lon, deposit, 0)

    part = 32
    lane = lax.broadcasted_iota(jnp.int32, (part, cols), 1)
    west, east = (lon + n_lon - 1) % n_lon, (lon + 1) % n_lon
    south, north = (lat + n_lat - 1) % n_lat, (lat + 1) % n_lat
    targets = ((lat, west), (lat, east), (south, lon), (north, lon))

    def edge_copy(step, side):
        return pltpu.make_async_remote_copy(
            src_ref=edge_out.at[step, side], dst_ref=edge_in.at[step, side],
            send_sem=edge_send_sem.at[step, side], recv_sem=edge_recv_sem.at[step, side],
            device_id=targets[side], device_id_type=MESH,
        )

    def split(s, w):
        flux = (0.5 * w) * s
        even = RATE * s
        return even + flux, even - flux

    for step in range(STEPS):
        src, dst = (state, later) if step % 2 == 0 else (later, state)

        edge_out[step, 2] = split(src[0], wlat[0])[0]
        edge_copy(step, 2).start()
        edge_out[step, 3] = split(src[rows - 1], wlat[rows - 1])[1]
        edge_copy(step, 3).start()

        def pack(q, carry):
            at = pl.ds(pl.multiple_of(q * part, part), part)

            def one(r, packed):
                plus, minus = split(src[r, at, :], wlon[r, at, :])
                return (
                    jnp.where(lane == r, pltpu.roll(plus, r, 1), packed[0]),
                    jnp.where(lane == r, pltpu.roll(minus, r + 1, 1), packed[1]),
                )

            zero = jnp.zeros((part, cols), jnp.float32)
            packed = lax.fori_loop(0, rows, one, (zero, zero))
            edge_out[step, 0, at, :] = packed[0]
            edge_out[step, 1, at, :] = packed[1]
            return carry

        lax.fori_loop(0, levels // part, pack, 0)
        edge_copy(step, 0).start()
        edge_copy(step, 1).start()

        def inner(r, carry):
            above, below = jnp.minimum(r + 1, rows - 1), jnp.maximum(r - 1, 0)
            for q in range(levels // part):
                at = pl.ds(q * part, part)
                s = src[r, at, :]
                plus, minus = split(s, wlon[r, at, :])
                from_north = split(src[above, at, :], wlat[above, at, :])[0]
                from_south = split(src[below, at, :], wlat[below, at, :])[1]
                dst[r, at, :] = (
                    (1.0 - 4.0 * RATE) * s
                    + jnp.where(lane == cols - 1, 0.0, pltpu.roll(plus, cols - 1, 1))
                    + jnp.where(lane == 0, 0.0, pltpu.roll(minus, 1, 1))
                    + jnp.where(r < rows - 1, from_north, 0.0)
                    + jnp.where(r > 0, from_south, 0.0)
                )
            return carry

        lax.fori_loop(0, rows, inner, 0)

        edge_copy(step, 2).wait()
        edge_copy(step, 3).wait()
        dst[rows - 1] = dst[rows - 1] + jnp.where(lat < n_lat - 1, edge_in[step, 2], 0.0)
        dst[0] = dst[0] + jnp.where(lat > 0, edge_in[step, 3], 0.0)
        edge_copy(step, 0).wait()
        edge_copy(step, 1).wait()
        last = step == STEPS - 1

        def mend(r, carry):
            for q in range(levels // part):
                at = pl.ds(q * part, part)
                from_east = pltpu.roll(edge_in[step, 0, at, :], cols - 1 - r, 1)
                from_west = pltpu.roll(edge_in[step, 1, at, :], (cols - r) % cols, 1)
                dst[r, at, :] = dst[r, at, :] + jnp.where(
                    lane == cols - 1, from_east, jnp.where(lane == 0, from_west, 0.0)
                )
            if last:
                pltpu.make_async_copy(dst.at[r], out_hbm.at[:, r, :], out_sem).start()
            return carry

        lax.fori_loop(0, rows, mend, 0)

    final = state if STEPS % 2 == 0 else later
    pltpu.make_async_copy(final, final, out_sem).wait()

    def drain(i, carry):
        @pl.when(i != (n_lon - 1) * n_lat)
        def _():
            pltpu.make_async_remote_copy(
                src_ref=send.at[i], dst_ref=recv.at[i],
                send_sem=send_sem.at[i], recv_sem=recv_sem.at[i],
                device_id=(north, lon), device_id_type=MESH,
            ).wait_send()
        return carry

    lax.fori_loop(0, n_dev, drain, 0)


def local(departures, footprint, channel_map, adjoint_in, wind_lon, wind_lat):
    n_lat, n_lon = lax.axis_size("lat"), lax.axis_size("lon")
    n_dev = n_lat * n_lon
    levels, rows, cols = adjoint_in.shape
    obs = departures.shape[0]
    capacity = 2 * obs // n_dev
    slots = -(-capacity // LANES) * LANES
    block = (n_dev, levels + META, slots)
    field = pltpu.VMEM((rows, levels, cols), jnp.float32)
    vmem, anywhere = pl.BlockSpec(memory_space=pltpu.VMEM), pl.BlockSpec(memory_space=pl.ANY)
    return pl.pallas_call(
        functools.partial(kernel, n_lat, n_lon),
        out_shape=jax.ShapeDtypeStruct(adjoint_in.shape, jnp.float32),
        in_specs=[vmem] * 3 + [anywhere] * 3,
        out_specs=anywhere,
        scratch_shapes=[
            pltpu.VMEM((levels + META, obs), jnp.bfloat16),
            pltpu.VMEM((8, obs), jnp.int32),
            pltpu.VMEM(block, jnp.bfloat16),
            pltpu.VMEM(block, jnp.bfloat16),
            field, field, field, field,
            pltpu.VMEM((STEPS, 4, levels, cols), jnp.float32),
            pltpu.VMEM((STEPS, 4, levels, cols), jnp.float32),
            pltpu.SemaphoreType.DMA((3,)),
            pltpu.SemaphoreType.DMA,
            pltpu.SemaphoreType.DMA((n_dev,)),
            pltpu.SemaphoreType.DMA((n_dev,)),
            pltpu.SemaphoreType.DMA((STEPS, 4)),
            pltpu.SemaphoreType.DMA((STEPS, 4)),
        ],
        compiler_params=pltpu.CompilerParams(
            collective_id=0, has_side_effects=True, vmem_limit_bytes=48 << 20
        ),
        name="assimilate",
    )(footprint.T, departures, channel_map.T, adjoint_in, wind_lon, wind_lat)


def solution(mesh):
    in_specs = (
        P(("lat", "lon"), None),
        P(("lat", "lon"), None),
        P(),
        P(None, "lat", "lon"),
        P(None, "lat", "lon"),
        P(None, "lat", "lon"),
    )
    out_specs = P(None, "lat", "lon")
    return jax.shard_map(local, mesh=mesh, in_specs=in_specs, out_specs=out_specs, check_vma=False)
```

```python
import functools

import jax
import jax.numpy as jnp
from jax import lax
from jax.experimental import pallas as pl
from jax.experimental.pallas import tpu as pltpu
from jax.sharding import PartitionSpec as P

STEPS = 2
RATE = 0.2
LANES = 128
META = 16
MESH = pl.DeviceIdType.MESH


def log2(size):
    assert size & (size - 1) == 0
    return size.bit_length() - 1


def nt_dot(a, b):
    return lax.dot_general(a, b, (((1,), (1,)), ((), ())), preferred_element_type=jnp.float32)


def kernel(
    n_lat, n_lon, foot, dep_hbm, cmap, adj_hbm, wlon_hbm, wlat_hbm, out_hbm,
    dep, prof, tag, send, recv, state, later, wlon, wlat, edge_out, edge_in,
    load_sem, out_sem, send_sem, recv_sem, edge_send_sem, edge_recv_sem,
):
    lat, lon = lax.axis_index("lat"), lax.axis_index("lon")
    n_dev = n_lat * n_lon
    rows, levels, cols = state.shape
    obs = dep.shape[0]
    slots = recv.shape[2]

    barrier = pltpu.get_barrier_semaphore()

    def greet(i, carry):
        pl.semaphore_signal(
            barrier, inc=1,
            device_id=((lat + i // n_lon) % n_lat, (lon + i % n_lon) % n_lon),
            device_id_type=MESH,
        )
        return carry

    lax.fori_loop(1, n_dev, greet, 0)

    pltpu.make_async_copy(dep_hbm, dep, load_sem.at[3]).start()

    def load(r, carry):
        pltpu.make_async_copy(adj_hbm.at[:, r, :], state.at[r], load_sem.at[0]).start()
        pltpu.make_async_copy(wlon_hbm.at[:, r, :], wlon.at[r], load_sem.at[1]).start()
        pltpu.make_async_copy(wlat_hbm.at[:, r, :], wlat.at[r], load_sem.at[2]).start()
        return carry

    lax.fori_loop(0, rows, load, 0)

    shift_grid, shift_row, shift_col = log2(n_lon * cols), log2(rows), log2(cols)
    cells = foot[...]
    grid_row = lax.shift_right_logical(cells, shift_grid)
    grid_col = cells & (n_lon * cols - 1)
    owner = (
        lax.shift_right_logical(grid_row[0:1], shift_row) * n_lon
        + lax.shift_right_logical(grid_col[0:1], shift_col)
    )
    in_row = grid_row & (rows - 1)
    in_col = grid_col & (cols - 1)

    def base(cell):
        low = jnp.minimum(jnp.minimum(cell[0:1], cell[1:2]), jnp.minimum(cell[2:3], cell[3:4]))
        high = jnp.maximum(jnp.maximum(cell[0:1], cell[1:2]), jnp.maximum(cell[2:3], cell[3:4]))
        return jnp.where(high - low == 1, low, high)

    base_row, base_col = base(in_row), base(in_col)
    chunk = 256
    upper = jnp.where(
        lax.broadcasted_iota(jnp.int32, (chunk, chunk), 0)
        <= lax.broadcasted_iota(jnp.int32, (chunk, chunk), 1),
        1.0, 0.0,
    ).astype(jnp.bfloat16)
    owners = lax.broadcasted_iota(jnp.int32, (n_dev, chunk), 0)
    seen = jnp.zeros((n_dev, 1), jnp.float32)
    for start in range(0, obs, chunk):
        hot = jnp.where(owners == owner[:, start:start + chunk], 1.0, 0.0)
        count = jnp.dot(hot.astype(jnp.bfloat16), upper, preferred_element_type=jnp.float32) + seen
        place = jnp.sum(hot * count, axis=0, keepdims=True) - 1.0
        seen = count[:, chunk - 1:chunk]
        tag[0:1, start:start + chunk] = place.astype(jnp.int32)
    tag[1:2, :] = owner

    pltpu.make_async_copy(dep_hbm, dep, load_sem.at[3]).wait()
    prof[0:levels, :] = lax.dot_general(
        cmap[...], dep[...], (((0,), (1,)), ((), ())), preferred_element_type=jnp.float32
    ).astype(jnp.bfloat16)
    which = lax.broadcasted_iota(jnp.int32, (META, obs), 0)
    prof[levels:levels + META, :] = jnp.where(
        which == 0, base_row, jnp.where(which == 1, base_col, 0)
    ).astype(jnp.float32).astype(jnp.bfloat16)

    pl.semaphore_wait(barrier, n_dev - 1)

    def place_of(k):
        return k // 2 + (k % 2) * (n_lon - 1 - 2 * (k // 2))

    own = 1

    def away(k):
        k = place_of(k)
        step = (k + 1) // 2
        return (n_lon // 2 + n_lon + step * (1 - 2 * (k % 2))) % n_lon

    def transfer(i, a, k):
        return pltpu.make_async_remote_copy(
            src_ref=send.at[i], dst_ref=recv.at[i],
            send_sem=send_sem.at[i], recv_sem=recv_sem.at[i],
            device_id=((lat + a) % n_lat, (lon + away(k)) % n_lon),
            device_id_type=MESH,
        )

    def route(k, carry):
        place, owner = tag[0:1, :], tag[1:2, :]
        slot = lax.broadcasted_iota(jnp.int32, (slots, obs), 0)
        hots = []
        for a in range(n_lat):
            target = (lat + a) % n_lat * n_lon + (lon + away(k)) % n_lon
            wanted = jnp.where(owner == target, place, -1)
            hots.append(jnp.where(slot == wanted, 1.0, 0.0).astype(jnp.bfloat16))
        blocks = nt_dot(prof[...], jnp.concatenate(hots, axis=0)).astype(jnp.bfloat16)
        for a in range(n_lat):
            i = k * n_lat + a
            block = blocks[:, a * slots:(a + 1) * slots]
            if a == 0:
                @pl.when(k == own)
                def _():
                    recv[i] = block

                @pl.when(k != own)
                def _():
                    send[i] = block
                    transfer(i, a, k).start()
            else:
                send[i] = block
                transfer(i, a, k).start()
        return carry

    lax.fori_loop(0, n_lon, route, 0)

    later[...] = jnp.zeros_like(later)
    for which, buf in enumerate((state, wlon, wlat)):
        pltpu.make_async_copy(buf, buf, load_sem.at[which]).wait()

    tile = 8
    depth = n_lat * slots

    def deposit(k, carry):
        for a in range(n_lat):
            if a == 0:
                @pl.when(k != own)
                def _():
                    transfer(k * n_lat, 0, k).wait_recv()
            else:
                transfer(k * n_lat + a, a, k).wait_recv()
        parts = [recv[k * n_lat + a] for a in range(n_lat)]
        got = jnp.concatenate([p[0:levels] for p in parts], axis=1)
        meta = jnp.concatenate([p[levels:levels + META] for p in parts], axis=1)
        meta = meta.astype(jnp.float32).astype(jnp.int32)
        at_row, at_col = meta[0:1], meta[1:2]
        cell = lax.broadcasted_iota(jnp.int32, (2 * cols, depth), 0)
        first = at_row % 2 * cols
        cell_hot = jnp.where(
            (cell == first + at_col) | (cell == first + ((at_col + 1) & (cols - 1))), 0.25, 0.0
        ).astype(jnp.bfloat16)
        pair = lax.shift_right_logical(at_row, 1)
        stacked = got.reshape(levels // 16, 16, depth)

        def rows_of(t, carry):
            lhs = []
            for j in range(tile):
                hot = jnp.where(pair == t * tile + j, 1.0, 0.0)
                hot = jnp.broadcast_to(hot, (16, depth)).astype(jnp.bfloat16)
                lhs.append((stacked * hot[None]).reshape(levels, depth))
            out = nt_dot(jnp.concatenate(lhs, axis=0), cell_hot)
            for j in range(tile):
                r = 2 * (t * tile + j)
                here = out[j * levels:(j + 1) * levels]
                later[r] = later[r] + here[:, 0:cols]
                later[r + 1] = later[r + 1] + here[:, cols:2 * cols]
            return carry

        lax.fori_loop(0, rows // 2 // tile, rows_of, 0)
        return carry

    lax.fori_loop(0, n_lon, deposit, 0)

    part = 16
    assert 2 * rows <= cols and rows % 4 == 0
    lane = lax.broadcasted_iota(jnp.int32, (part, cols), 1)
    all_lane = lax.broadcasted_iota(jnp.int32, (levels, cols), 1)
    side_half = jnp.where(lane == cols - 1, -0.5, 0.5)
    west, east = (lon + n_lon - 1) % n_lon, (lon + 1) % n_lon
    south, north = (lat + n_lat - 1) % n_lat, (lat + 1) % n_lat
    targets = ((lat, west), (lat, east), (south, lon), (north, lon))

    def edge_copy(step, side):
        return pltpu.make_async_remote_copy(
            src_ref=edge_out.at[step, max(side, 1)], dst_ref=edge_in.at[step, side],
            send_sem=edge_send_sem.at[step, side], recv_sem=edge_recv_sem.at[step, side],
            device_id=targets[side], device_id_type=MESH,
        )

    def split(s, w):
        flux = (0.5 * w) * s
        even = RATE * s
        return even + flux, even - flux

    def pack_row(packed, r, s, w):
        side = (RATE + side_half * w) * s
        if r > 0:
            side = pltpu.roll(side, 2 * r, 1)
        return jnp.where((lane == 2 * r) | (lane == (2 * r - 1) % cols), side, packed)

    def part_at(q):
        return pl.ds(pl.multiple_of(q * part, part), part)

    def pack(q, carry):
        at = part_at(q)
        packed = jnp.zeros((part, cols), jnp.float32)
        below = later[rows - 1, at, :]
        for r in range(rows):
            here = later[r, at, :]
            s = state[r, at, :] + (here + below)
            state[r, at, :] = s
            packed = pack_row(packed, r, s, wlon[r, at, :])
            below = here
        edge_out[0, 1, at, :] = packed
        return carry

    lax.fori_loop(0, levels // part, pack, 0)
    edge_copy(0, 0).start()
    edge_copy(0, 1).start()
    edge_out[0, 2] = split(state[0], wlat[0])[0]
    edge_out[0, 3] = split(state[rows - 1], wlat[rows - 1])[1]
    edge_copy(0, 2).start()
    edge_copy(0, 3).start()

    for step in range(STEPS):
        src, dst = (state, later) if step % 2 == 0 else (later, state)
        last = step == STEPS - 1

        def inner(q, carry):
            at = part_at(q)
            centre = below = None
            for r in range(rows + 1):
                above = None
                if r < rows:
                    s = src[r, at, :]
                    plus, minus = split(s, wlon[r, at, :])
                    across = (
                        (1.0 - 4.0 * RATE) * s
                        + jnp.where(lane == cols - 1, 0.0, pltpu.roll(plus, cols - 1, 1))
                        + jnp.where(lane == 0, 0.0, pltpu.roll(minus, 1, 1))
                    )
                    above, here = split(s, wlat[r, at, :])
                if r > 0:
                    total = centre
                    if above is not None:
                        total = total + above
                    dst[r - 1, at, :] = total
                if r < rows:
                    centre = across if below is None else across + below
                    below = here
            return carry

        lax.fori_loop(0, levels // part, inner, 0)

        for side in range(4):
            edge_copy(step, side).wait()
        from_north = jnp.where(lat < n_lat - 1, edge_in[step, 2], 0.0)
        from_south = jnp.where(lat > 0, edge_in[step, 3], 0.0)
        dst[rows - 1] = dst[rows - 1] + from_north
        dst[0] = dst[0] + from_south
        edge_in[step, 0] = jnp.where(
            all_lane % 2 == 0, edge_in[step, 0], pltpu.roll(edge_in[step, 1], 2, 1)
        )

        if not last:
            def mend(q, carry):
                at = part_at(q)
                packed = jnp.zeros((part, cols), jnp.float32)
                both = edge_in[step, 0, at, :]
                for r in range(rows):
                    moved = pltpu.roll(both, cols - 1 - 2 * r, 1)
                    s = dst[r, at, :] + jnp.where((lane == cols - 1) | (lane == 0), moved, 0.0)
                    dst[r, at, :] = s
                    packed = pack_row(packed, r, s, wlon[r, at, :])
                edge_out[step + 1, 1, at, :] = packed
                return carry

            lax.fori_loop(0, levels // part, mend, 0)
            edge_copy(step + 1, 0).start()
            edge_copy(step + 1, 1).start()
            edge_out[step + 1, 2] = split(dst[0], wlat[0])[0]
            edge_out[step + 1, 3] = split(dst[rows - 1], wlat[rows - 1])[1]
            edge_copy(step + 1, 2).start()
            edge_copy(step + 1, 3).start()
        else:
            def finish(t, carry):
                for j in range(4):
                    r = t * 4 + j
                    for q in range(levels // part):
                        at = pl.ds(q * part, part)
                        moved = pltpu.roll(edge_in[step, 0, at, :], cols - 1 - 2 * r, 1)
                        dst[r, at, :] = dst[r, at, :] + jnp.where(
                            (lane == cols - 1) | (lane == 0), moved, 0.0
                        )
                    pltpu.make_async_copy(dst.at[r], out_hbm.at[:, r, :], out_sem).start()
                return carry

            lax.fori_loop(0, rows // 4, finish, 0)

    final = state if STEPS % 2 == 0 else later
    pltpu.make_async_copy(final, final, out_sem).wait()

    def drain(i, carry):
        @pl.when(i != own * n_lat)
        def _():
            pltpu.make_async_remote_copy(
                src_ref=send.at[i], dst_ref=recv.at[i],
                send_sem=send_sem.at[i], recv_sem=recv_sem.at[i],
                device_id=(north, lon), device_id_type=MESH,
            ).wait_send()
        return carry

    lax.fori_loop(0, n_dev, drain, 0)


def local(departures, footprint, channel_map, adjoint_in, wind_lon, wind_lat):
    n_lat, n_lon = lax.axis_size("lat"), lax.axis_size("lon")
    n_dev = n_lat * n_lon
    levels, rows, cols = adjoint_in.shape
    obs = departures.shape[0]
    capacity = 2 * obs // n_dev
    slots = -(-capacity // LANES) * LANES
    block = (n_dev, levels + META, slots)
    field = pltpu.VMEM((rows, levels, cols), jnp.float32)
    vmem, anywhere = pl.BlockSpec(memory_space=pltpu.VMEM), pl.BlockSpec(memory_space=pl.ANY)
    hbm = pl.BlockSpec(memory_space=pltpu.HBM)
    return pl.pallas_call(
        functools.partial(kernel, n_lat, n_lon),
        out_shape=jax.ShapeDtypeStruct(adjoint_in.shape, jnp.float32),
        in_specs=[vmem, hbm, vmem] + [hbm] * 3,
        out_specs=anywhere,
        scratch_shapes=[
            pltpu.VMEM(departures.shape, jnp.bfloat16),
            pltpu.VMEM((levels + META, obs), jnp.bfloat16),
            pltpu.VMEM((8, obs), jnp.int32),
            pltpu.VMEM(block, jnp.bfloat16),
            pltpu.VMEM(block, jnp.bfloat16),
            field, field, field, field,
            pltpu.VMEM((STEPS, 4, levels, cols), jnp.float32),
            pltpu.VMEM((STEPS, 4, levels, cols), jnp.float32),
            pltpu.SemaphoreType.DMA((4,)),
            pltpu.SemaphoreType.DMA,
            pltpu.SemaphoreType.DMA((n_dev,)),
            pltpu.SemaphoreType.DMA((n_dev,)),
            pltpu.SemaphoreType.DMA((STEPS, 4)),
            pltpu.SemaphoreType.DMA((STEPS, 4)),
        ],
        compiler_params=pltpu.CompilerParams(
            collective_id=0, has_side_effects=True, vmem_limit_bytes=62 << 20
        ),
        name="assimilate",
    )(footprint.T, departures, channel_map, adjoint_in, wind_lon, wind_lat)


def solution(mesh):
    in_specs = (
        P(("lat", "lon"), None),
        P(("lat", "lon"), None),
        P(),
        P(None, "lat", "lon"),
        P(None, "lat", "lon"),
        P(None, "lat", "lon"),
    )
    out_specs = P(None, "lat", "lon")
    return jax.shard_map(local, mesh=mesh, in_specs=in_specs, out_specs=out_specs, check_vma=False)
```

```python
import functools

import jax
import jax.numpy as jnp
from jax import lax
from jax.experimental import pallas as pl
from jax.experimental.pallas import tpu as pltpu
from jax.sharding import PartitionSpec as P

STEPS = 2
RATE = 0.2
LANES = 128
META = 8
MESH = pl.DeviceIdType.MESH


def log2(size):
    assert size & (size - 1) == 0
    return size.bit_length() - 1


def nt_dot(a, b):
    return lax.dot_general(a, b, (((1,), (1,)), ((), ())), preferred_element_type=jnp.float32)


def kernel(
    n_lat, n_lon, foot, dep_hbm, cmap, adj_hbm, wlon_hbm, wlat_hbm, out_hbm,
    dep, prof, tag, send, recv, state, later, wlon, wlat, edge_out, edge_in, fringe,
    load_sem, out_sem, send_sem, recv_sem, edge_send_sem, edge_recv_sem,
):
    lat, lon = lax.axis_index("lat"), lax.axis_index("lon")
    n_dev = n_lat * n_lon
    rows, levels, cols = state.shape
    obs = dep.shape[0]
    slots = recv.shape[2]

    barrier = pltpu.get_barrier_semaphore()

    def greet(i, carry):
        pl.semaphore_signal(
            barrier, inc=1,
            device_id=((lat + i // n_lon) % n_lat, (lon + i % n_lon) % n_lon),
            device_id_type=MESH,
        )
        return carry

    lax.fori_loop(1, n_dev, greet, 0)

    pltpu.make_async_copy(dep_hbm, dep, load_sem.at[3]).start()

    def load(r, carry):
        pltpu.make_async_copy(adj_hbm.at[:, r, :], state.at[r], load_sem.at[0]).start()
        pltpu.make_async_copy(wlon_hbm.at[:, r, :], wlon.at[r], load_sem.at[1]).start()
        pltpu.make_async_copy(wlat_hbm.at[:, r, :], wlat.at[r], load_sem.at[2]).start()
        return carry

    lax.fori_loop(0, rows, load, 0)

    shift_grid, shift_row, shift_col = log2(n_lon * cols), log2(rows), log2(cols)
    cells = foot[...]
    grid_row = lax.shift_right_logical(cells, shift_grid)
    grid_col = cells & (n_lon * cols - 1)
    owner = (
        lax.shift_right_logical(grid_row[0:1], shift_row) * n_lon
        + lax.shift_right_logical(grid_col[0:1], shift_col)
    )
    in_row = grid_row & (rows - 1)
    in_col = grid_col & (cols - 1)

    def base(cell):
        low = jnp.minimum(jnp.minimum(cell[0:1], cell[1:2]), jnp.minimum(cell[2:3], cell[3:4]))
        high = jnp.maximum(jnp.maximum(cell[0:1], cell[1:2]), jnp.maximum(cell[2:3], cell[3:4]))
        return jnp.where(high - low == 1, low, high)

    base_row, base_col = base(in_row), base(in_col)
    chunk = 256
    upper = jnp.where(
        lax.broadcasted_iota(jnp.int32, (chunk, chunk), 0)
        <= lax.broadcasted_iota(jnp.int32, (chunk, chunk), 1),
        1.0, 0.0,
    ).astype(jnp.bfloat16)
    owners = lax.broadcasted_iota(jnp.int32, (n_dev, chunk), 0)
    seen = jnp.zeros((n_dev, 1), jnp.float32)
    for start in range(0, obs, chunk):
        hot = jnp.where(owners == owner[:, start:start + chunk], 1.0, 0.0)
        count = jnp.dot(hot.astype(jnp.bfloat16), upper, preferred_element_type=jnp.float32) + seen
        place = jnp.sum(hot * count, axis=0, keepdims=True) - 1.0
        seen = count[:, chunk - 1:chunk]
        tag[0:1, start:start + chunk] = place.astype(jnp.int32)
    tag[1:2, :] = owner

    pltpu.make_async_copy(dep_hbm, dep, load_sem.at[3]).wait()
    prof[0:levels, :] = lax.dot_general(
        cmap[...], dep[...], (((0,), (1,)), ((), ())), preferred_element_type=jnp.float32
    ).astype(jnp.bfloat16)
    which = lax.broadcasted_iota(jnp.int32, (META, obs), 0)
    prof[levels:levels + META, :] = jnp.where(
        which == 0, base_row, jnp.where(which == 1, base_col, 0)
    ).astype(jnp.float32).astype(jnp.bfloat16)

    pl.semaphore_wait(barrier, n_dev - 1)

    def place_of(k):
        return k // 2 + (k % 2) * (n_lon - 1 - 2 * (k // 2))

    own = 1

    def away(k):
        k = place_of(k)
        step = (k + 1) // 2
        return (n_lon // 2 + n_lon + step * (1 - 2 * (k % 2))) % n_lon

    def transfer(i, a, k):
        return pltpu.make_async_remote_copy(
            src_ref=send.at[i], dst_ref=recv.at[i],
            send_sem=send_sem.at[i], recv_sem=recv_sem.at[i],
            device_id=((lat + a) % n_lat, (lon + away(k)) % n_lon),
            device_id_type=MESH,
        )

    def route(k, carry):
        place, owner = tag[0:1, :], tag[1:2, :]
        slot = lax.broadcasted_iota(jnp.int32, (slots, obs), 0)
        hots = []
        for a in range(n_lat):
            target = (lat + a) % n_lat * n_lon + (lon + away(k)) % n_lon
            wanted = jnp.where(owner == target, place, -1)
            hots.append(jnp.where(slot == wanted, 1.0, 0.0).astype(jnp.bfloat16))
        blocks = nt_dot(prof[...], jnp.concatenate(hots, axis=0)).astype(jnp.bfloat16)
        for a in range(n_lat):
            i = k * n_lat + a
            block = blocks[:, a * slots:(a + 1) * slots]
            if a == 0:
                @pl.when(k == own)
                def _():
                    recv[i] = block

                @pl.when(k != own)
                def _():
                    send[i] = block
                    transfer(i, a, k).start()
            else:
                send[i] = block
                transfer(i, a, k).start()
        return carry

    lax.fori_loop(0, n_lon, route, 0)

    later[...] = jnp.zeros_like(later)
    for which, buf in enumerate((state, wlon, wlat)):
        pltpu.make_async_copy(buf, buf, load_sem.at[which]).wait()

    tile = 8
    depth = n_lat * slots

    def deposit(k, carry):
        for a in range(n_lat):
            if a == 0:
                @pl.when(k != own)
                def _():
                    transfer(k * n_lat, 0, k).wait_recv()
            else:
                transfer(k * n_lat + a, a, k).wait_recv()
        parts = [recv[k * n_lat + a] for a in range(n_lat)]
        got = jnp.concatenate([p[0:levels] for p in parts], axis=1)
        meta = jnp.concatenate([p[levels:levels + META] for p in parts], axis=1)
        meta = meta.astype(jnp.float32).astype(jnp.int32)
        at_row, at_col = meta[0:1], meta[1:2]
        cell = lax.broadcasted_iota(jnp.int32, (2 * cols, depth), 0)
        first = at_row % 2 * cols
        cell_hot = jnp.where(
            (cell == first + at_col) | (cell == first + ((at_col + 1) & (cols - 1))), 0.25, 0.0
        ).astype(jnp.bfloat16)
        pair = lax.shift_right_logical(at_row, 1)
        stacked = got.reshape(levels // 16, 16, depth)

        def rows_of(t, carry):
            lhs = []
            for j in range(tile):
                hot = jnp.where(pair == t * tile + j, 1.0, 0.0)
                hot = jnp.broadcast_to(hot, (16, depth)).astype(jnp.bfloat16)
                lhs.append((stacked * hot[None]).reshape(levels, depth))
            out = nt_dot(jnp.concatenate(lhs, axis=0), cell_hot)
            for j in range(tile):
                r = 2 * (t * tile + j)
                here = out[j * levels:(j + 1) * levels]
                later[r] = later[r] + here[:, 0:cols]
                later[r + 1] = later[r + 1] + here[:, cols:2 * cols]
            return carry

        lax.fori_loop(0, rows // 2 // tile, rows_of, 0)
        return carry

    lax.fori_loop(0, n_lon, deposit, 0)

    part = 16
    assert 2 * rows <= cols and rows % 4 == 0
    lane = lax.broadcasted_iota(jnp.int32, (part, cols), 1)
    all_lane = lax.broadcasted_iota(jnp.int32, (levels, cols), 1)
    side_half = jnp.where(lane == cols - 1, -0.5, 0.5)
    west, east = (lon + n_lon - 1) % n_lon, (lon + 1) % n_lon
    south, north = (lat + n_lat - 1) % n_lat, (lat + 1) % n_lat
    targets = ((lat, west), (lat, east), (south, lon), (north, lon))

    def edge_copy(step, side):
        return pltpu.make_async_remote_copy(
            src_ref=edge_out.at[step, max(side, 1)], dst_ref=edge_in.at[step, side],
            send_sem=edge_send_sem.at[step, side], recv_sem=edge_recv_sem.at[step, side],
            device_id=targets[side], device_id_type=MESH,
        )

    def split(s, w):
        flux = (0.5 * w) * s
        even = RATE * s
        return even + flux, even - flux

    def pack_row(packed, r, s, w):
        side = (RATE + side_half * w) * s
        if r > 0:
            side = pltpu.roll(side, 2 * r, 1)
        return jnp.where((lane == 2 * r) | (lane == (2 * r - 1) % cols), side, packed)

    def part_at(q):
        return pl.ds(pl.multiple_of(q * part, part), part)

    def pack(q, carry):
        at = part_at(q)
        packed = jnp.zeros((part, cols), jnp.float32)
        below = later[rows - 1, at, :]
        for r in range(rows):
            here = later[r, at, :]
            s = state[r, at, :] + (here + below)
            state[r, at, :] = s
            packed = pack_row(packed, r, s, wlon[r, at, :])
            below = here
        edge_out[0, 1, at, :] = packed.astype(jnp.bfloat16)
        return carry

    def send_rows(step, first, final):
        edge_out[step, 2] = split(first, wlat[0])[0].astype(jnp.bfloat16)
        edge_out[step, 3] = split(final, wlat[rows - 1])[1].astype(jnp.bfloat16)

        @pl.when(lat > 0)
        def _():
            edge_copy(step, 2).start()

        @pl.when(lat < n_lat - 1)
        def _():
            edge_copy(step, 3).start()

    def await_rows(step):
        @pl.when(lat > 0)
        def _():
            edge_copy(step, 2).wait_send()
            edge_copy(step, 3).wait_recv()

        @pl.when(lat < n_lat - 1)
        def _():
            edge_copy(step, 3).wait_send()
            edge_copy(step, 2).wait_recv()

    send_rows(
        0,
        state[0] + (later[0] + later[rows - 1]),
        state[rows - 1] + (later[rows - 1] + later[rows - 2]),
    )
    lax.fori_loop(0, levels // part, pack, 0)
    edge_copy(0, 0).start()
    edge_copy(0, 1).start()

    for step in range(STEPS):
        src, dst = (state, later) if step % 2 == 0 else (later, state)
        last = step == STEPS - 1

        def inner(q, carry):
            at = part_at(q)
            centre = below = None
            for r in range(rows + 1):
                above = None
                if r < rows:
                    s = src[r, at, :]
                    plus, minus = split(s, wlon[r, at, :])
                    across = (
                        (1.0 - 4.0 * RATE) * s
                        + jnp.where(lane == cols - 1, 0.0, pltpu.roll(plus, cols - 1, 1))
                        + jnp.where(lane == 0, 0.0, pltpu.roll(minus, 1, 1))
                    )
                    above, here = split(s, wlat[r, at, :])
                if r > 0:
                    total = centre
                    if above is not None:
                        total = total + above
                    dst[r - 1, at, :] = total
                if r < rows:
                    centre = across if below is None else across + below
                    below = here
            return carry

        lax.fori_loop(0, levels // part, inner, 0)

        await_rows(step)

        @pl.when(lat < n_lat - 1)
        def _():
            dst[rows - 1] = dst[rows - 1] + edge_in[step, 2].astype(jnp.float32)

        @pl.when(lat > 0)
        def _():
            dst[0] = dst[0] + edge_in[step, 3].astype(jnp.float32)

        edge_copy(step, 0).wait()
        edge_copy(step, 1).wait()
        both = jnp.where(
            all_lane % 2 == 0,
            edge_in[step, 0].astype(jnp.float32),
            pltpu.roll(edge_in[step, 1].astype(jnp.float32), 2, 1),
        )
        fringe[...] = both
        at_side = (all_lane == cols - 1) | (all_lane == 0)

        if not last:
            def mend(q, carry):
                at = part_at(q)
                packed = jnp.zeros((part, cols), jnp.float32)
                both = fringe[at, :]
                for r in range(rows):
                    moved = pltpu.roll(both, cols - 1 - 2 * r, 1)
                    s = dst[r, at, :] + jnp.where((lane == cols - 1) | (lane == 0), moved, 0.0)
                    dst[r, at, :] = s
                    packed = pack_row(packed, r, s, wlon[r, at, :])
                edge_out[step + 1, 1, at, :] = packed.astype(jnp.bfloat16)
                return carry

            send_rows(
                step + 1,
                dst[0] + jnp.where(at_side, pltpu.roll(both, cols - 1, 1), 0.0),
                dst[rows - 1]
                + jnp.where(at_side, pltpu.roll(both, cols - 1 - 2 * (rows - 1), 1), 0.0),
            )
            lax.fori_loop(0, levels // part, mend, 0)
            edge_copy(step + 1, 0).start()
            edge_copy(step + 1, 1).start()
        else:
            def finish(t, carry):
                for j in range(4):
                    r = t * 4 + j
                    for q in range(levels // part):
                        at = pl.ds(q * part, part)
                        moved = pltpu.roll(fringe[at, :], cols - 1 - 2 * r, 1)
                        dst[r, at, :] = dst[r, at, :] + jnp.where(
                            (lane == cols - 1) | (lane == 0), moved, 0.0
                        )
                    pltpu.make_async_copy(dst.at[r], out_hbm.at[:, r, :], out_sem).start()
                return carry

            lax.fori_loop(0, rows // 4, finish, 0)

    final = state if STEPS % 2 == 0 else later
    pltpu.make_async_copy(final, final, out_sem).wait()

    def drain(i, carry):
        @pl.when(i != own * n_lat)
        def _():
            pltpu.make_async_remote_copy(
                src_ref=send.at[i], dst_ref=recv.at[i],
                send_sem=send_sem.at[i], recv_sem=recv_sem.at[i],
                device_id=(north, lon), device_id_type=MESH,
            ).wait_send()
        return carry

    lax.fori_loop(0, n_dev, drain, 0)


def local(departures, footprint, channel_map, adjoint_in, wind_lon, wind_lat):
    n_lat, n_lon = lax.axis_size("lat"), lax.axis_size("lon")
    n_dev = n_lat * n_lon
    levels, rows, cols = adjoint_in.shape
    obs = departures.shape[0]
    capacity = 2 * obs // n_dev
    slots = -(-capacity // LANES) * LANES
    block = (n_dev, levels + META, slots)
    field = pltpu.VMEM((rows, levels, cols), jnp.float32)
    vmem, anywhere = pl.BlockSpec(memory_space=pltpu.VMEM), pl.BlockSpec(memory_space=pl.ANY)
    hbm = pl.BlockSpec(memory_space=pltpu.HBM)
    return pl.pallas_call(
        functools.partial(kernel, n_lat, n_lon),
        out_shape=jax.ShapeDtypeStruct(adjoint_in.shape, jnp.float32),
        in_specs=[vmem, hbm, vmem] + [hbm] * 3,
        out_specs=anywhere,
        scratch_shapes=[
            pltpu.VMEM(departures.shape, jnp.bfloat16),
            pltpu.VMEM((levels + META, obs), jnp.bfloat16),
            pltpu.VMEM((8, obs), jnp.int32),
            pltpu.VMEM(block, jnp.bfloat16),
            pltpu.VMEM(block, jnp.bfloat16),
            field, field, field, field,
            pltpu.VMEM((STEPS, 4, levels, cols), jnp.bfloat16),
            pltpu.VMEM((STEPS, 4, levels, cols), jnp.bfloat16),
            pltpu.VMEM((levels, cols), jnp.float32),
            pltpu.SemaphoreType.DMA((4,)),
            pltpu.SemaphoreType.DMA,
            pltpu.SemaphoreType.DMA((n_dev,)),
            pltpu.SemaphoreType.DMA((n_dev,)),
            pltpu.SemaphoreType.DMA((STEPS, 4)),
            pltpu.SemaphoreType.DMA((STEPS, 4)),
        ],
        compiler_params=pltpu.CompilerParams(
            collective_id=0, has_side_effects=True, vmem_limit_bytes=62 << 20
        ),
        name="assimilate",
    )(footprint.T, departures, channel_map, adjoint_in, wind_lon, wind_lat)


def solution(mesh):
    in_specs = (
        P(("lat", "lon"), None),
        P(("lat", "lon"), None),
        P(),
        P(None, "lat", "lon"),
        P(None, "lat", "lon"),
        P(None, "lat", "lon"),
    )
    out_specs = P(None, "lat", "lon")
    return jax.shard_map(local, mesh=mesh, in_specs=in_specs, out_specs=out_specs, check_vma=False)
```
